32 devices in a mesh: dp: 8 (over z, core), expert: 4 (over y, x).
Axes of the slice: x: 2, y: 2, z: 4, core: 2. Of those that a mesh axis runs over, the one named last changes fastest.
Arguments:
- tokens: bfloat16 [12288, 1024], P(('dp', 'expert')), may hold values from -6 to 6
- segments: int32 [12288], P(('dp', 'expert')), may hold values from 0 to 93, as said below
- routes: int32 [12288, 8], P(('dp', 'expert')), may hold values from 0 to 31, all different within a row; in each aligned block of 384 rows (0 to 383, 384 to 767, ...) at most 192 rows name the same one
- norm1_gain: bfloat16 [1024], P('dp'), may hold values from 0.5 to 1.5
- w_query: bfloat16 [1024, 1024], P('dp'), may hold values from -0.1875 to 0.1875
- key_projection: bfloat16 [1024, 512], P('dp'), may hold values from -0.1875 to 0.1875
- value_projection: bfloat16 [1024, 512], P('dp'), may hold values from -0.1875 to 0.1875
- w_output: bfloat16 [1024, 1024], P('dp'), may hold values from -1.5 to 1.5
- norm2_gain: bfloat16 [1024], P('dp'), may hold values from 0.5 to 1.5
- w_router: bfloat16 [1024, 32], P('dp'), may hold values from -0.1875 to 0.1875
- expert_gate: bfloat16 [32, 1024, 512], P('expert'), may hold values from -0.1875 to 0.1875
- expert_up: bfloat16 [32, 1024, 512], P('expert'), may hold values from -0.1875 to 0.1875
- expert_down: bfloat16 [32, 512, 1024], P('expert'), may hold values from -1 to 1
- cotangent: bfloat16 [12288, 1024], P(('dp', 'expert')), may hold values from -6 to 6
Outputs:
- output: bfloat16 [12288, 1024], P(('dp', 'expert'))
- grad_tokens: float32 [12288, 1024], P(('dp', 'expert'))
- grad_norm1: float32 [1024], P('dp')
- grad_query: float32 [1024, 1024], P('dp')
- grad_key: float32 [1024, 512], P('dp')
- grad_value: float32 [1024, 512], P('dp')
- grad_output_proj: float32 [1024, 1024], P('dp')
- grad_norm2: float32 [1024], P('dp')
- grad_router: float32 [1024, 32], P('dp')
- grad_expert_gate: float32 [32, 1024, 512], P('expert')
- grad_expert_up: float32 [32, 1024, 512], P('expert')
- grad_expert_down: float32 [32, 512, 1024], P('expert')
The draws below stay inside these ranges and needn't reach their ends.
Inputs may be any that keep to these rules, and one draw needn't show every extreme that they name: Segment numbers start at 0 and never fall; each segment lies inside one aligned block of 384 tokens (the tokens of one device). The first such block is a single segment; every other block holds exactly three segments, cut at positions drawn from the seed. `routes`: A token's 8 experts differ. Among the choices of one device's 384 tokens, no expert is named more than 192 times, a bound that some block reaches.
All inputs are finite; a program needn't handle non-finite values.
Results may differ from the reference program's by a relative error of at most 0.023.
Values may be sent and summed in bfloat16 or wider, within the bound.
No kernel may reach another device: no remote copies, remote signals or barrier semaphores. Data moves between devices by JAX's collectives and lax.ppermute only.
A program may use at most 320 MiB of HBM per device.

```python
import math
import jax
import jax.numpy as jnp
import numpy as np
from jax import lax

MODEL_DIMENSION = 1024
QUERY_HEADS = 16
KEY_VALUE_HEADS = 8
HEAD_DIMENSION = 64
FF = 512
EXPERTS = 32
TOP = 8
TOK_DEV = 384
TOKENS = 12288
CAP = 192


def draw_segments(key, part):
    block_count = TOKENS // TOK_DEV
    block_keys = jax.random.split(key, block_count)
    orders = jax.vmap(lambda k: jax.random.permutation(k, TOK_DEV - 1))(block_keys)
    cut_here = jnp.concatenate([jnp.zeros((block_count, 1), jnp.int32), (orders < 2).astype(jnp.int32)], axis=1)
    later_block = (jnp.arange(block_count, dtype=jnp.int32) >= 1).astype(jnp.int32)[:, None]
    cut_here = cut_here * later_block
    first_col = (jnp.arange(TOK_DEV, dtype=jnp.int32) == 0).astype(jnp.int32)[None, :]
    starts_here = jnp.maximum(cut_here, first_col).reshape(TOKENS)
    return (jnp.cumsum(starts_here) - 1).astype(jnp.int32)


def steps_of(own_key, shape, cuts, least, top_value):
    factor_of = 1.0
    for dim, shards_of in cuts:
        steps = jax.random.uniform(jax.random.fold_in(jax.random.fold_in(own_key, 6), dim), (shards_of,), jnp.float32, least / len(cuts), top_value / len(cuts))
        factor_of = factor_of * jnp.repeat(jnp.exp(steps), shape[dim] // shards_of).reshape((-1,) + (1,) * (len(shape) - 1 - dim))
    return factor_of


def routed_block(rng, own, number, rows, amount, top, bound, slope):
    sequence = jax.random.permutation(rng, amount)
    heavy_load, ordinary = portions_of(amount, rows * top, bound, slope, True), portions_of(amount, rows * top, bound, slope, False)
    places = jnp.arange(amount)

    def named(sizes, rotation):
        used = int((sizes > 0).sum())
        fixed = max(1, used // 4)
        passed = fixed + (places - fixed + rotation * (used - fixed)) % max(1, amount - fixed)
        return jnp.zeros((amount,), jnp.int32).at[sequence[jnp.where(places < fixed, places, passed)]].set(jnp.asarray(sizes, jnp.int32))

    sizes = jnp.where(number % 4 == 0, named(heavy_load, number // 4), named(ordinary, number - number // 4 - 1))
    mixed = jax.random.permutation(jax.random.fold_in(own, 3), amount)
    source_of, receiver = mixed[0:amount // 2 * 2:2], mixed[1:amount // 2 * 2:2]
    slack = jnp.minimum(sizes[source_of] - 1, bound - sizes[receiver]) // 2
    slack = jnp.where((source_of == sequence[0]) | (receiver == sequence[0]) | (sizes[receiver] == 0), 0, jnp.maximum(slack, 0))
    passed = jax.random.randint(jax.random.fold_in(own, 4), (amount // 2,), 0, 1 << 20) % (slack + 1)
    sizes = sizes.at[source_of].add(-passed).at[receiver].add(passed)
    labels = jnp.searchsorted(jnp.cumsum(sizes), jnp.arange(rows * top), side="right").astype(jnp.int32)
    table = labels.reshape(top, rows).T
    table = table[jax.random.permutation(jax.random.fold_in(own, 1), rows)]
    rotation = jax.random.randint(jax.random.fold_in(own, 2), (rows, 1), 0, top)
    return jnp.take_along_axis(table, (jnp.arange(top)[None, :] + rotation) % top, axis=1)


def portions_of(amount, total, reach, slope, full):
    portions = [(1 << 20) // math.isqrt(rank ** slope) + 1 for rank in range(1, amount + 1)]
    largest = reach if full else min(reach, max(-(-total // amount), total * portions[0] // sum(portions)))
    least = 1 if total - largest >= amount - 1 else 0
    holding, rest = [largest] + [least] * (amount - 1), total - largest - least * (amount - 1)
    while rest > 0:
        movable = [i for i in range(1, amount) if holding[i] < largest] or [i for i in range(1, amount) if holding[i] < reach]
        whole, left = sum([portions[i] for i in movable]), rest
        for i in movable:
            addition = min(reach - holding[i], max(1, left * portions[i] // whole), rest)
            holding[i] = holding[i] + addition
            rest = rest - addition
    return np.array(holding)


def bell_draw(stream_key, dims, spread, reach, shards=(), held_as=jnp.bfloat16):
    values = spread * jax.random.normal(stream_key, dims, jnp.float32)
    if shards:
        values = values * steps_of(stream_key, dims, shards, -0.22, 0.18)
    return jnp.clip(values, -reach, reach).astype(held_as)


def setup_inputs(seed: int = 0) -> dict:
    seeds = jax.random.split(jax.random.key(seed), 15)
    tokens = bell_draw(seeds[0], (TOKENS, MODEL_DIMENSION), 1.0, 6.0, ((0, 32),))
    segments = draw_segments(jax.random.fold_in(seeds[14], 71), 0)
    routes_keys = jax.random.split(jax.random.fold_in(seeds[2], 1), TOKENS // TOK_DEV)
    routes_turns = jax.random.permutation(jax.random.fold_in(seeds[2], 3), TOKENS // TOK_DEV)
    routes = jax.vmap(lambda own, number: routed_block(jax.random.fold_in(seeds[2], 2), own, number, TOK_DEV, EXPERTS, TOP, CAP, 2))(routes_keys, routes_turns).reshape((TOKENS, TOP))
    norm1_gain = jnp.clip(1.0 + 0.1 * jax.random.normal(seeds[3], (MODEL_DIMENSION,), jnp.float32), 0.5, 1.5).astype(jnp.bfloat16)
    w_query = bell_draw(seeds[4], (MODEL_DIMENSION, QUERY_HEADS * HEAD_DIMENSION), MODEL_DIMENSION ** -0.5, 0.1875, ((0, 8),))
    key_projection = bell_draw(seeds[5], (MODEL_DIMENSION, KEY_VALUE_HEADS * HEAD_DIMENSION), MODEL_DIMENSION ** -0.5, 0.1875, ((0, 8),))
    value_projection = bell_draw(seeds[6], (MODEL_DIMENSION, KEY_VALUE_HEADS * HEAD_DIMENSION), MODEL_DIMENSION ** -0.5, 0.1875, ((0, 8),))
    w_output = bell_draw(seeds[7], (QUERY_HEADS * HEAD_DIMENSION, MODEL_DIMENSION), (max(QUERY_HEADS * HEAD_DIMENSION // 64, 1)) ** -0.5, 1.5, ((0, 8),))
    norm2_gain = jnp.clip(1.0 + 0.1 * jax.random.normal(seeds[8], (MODEL_DIMENSION,), jnp.float32), 0.5, 1.5).astype(jnp.bfloat16)
    w_router = bell_draw(seeds[9], (MODEL_DIMENSION, EXPERTS), MODEL_DIMENSION ** -0.5, 0.1875, ((0, 8),))
    expert_gate = bell_draw(seeds[10], (EXPERTS, MODEL_DIMENSION, FF), MODEL_DIMENSION ** -0.5, 0.1875, ((0, 4),))
    expert_up = bell_draw(seeds[11], (EXPERTS, MODEL_DIMENSION, FF), MODEL_DIMENSION ** -0.5, 0.1875, ((0, 4),))
    expert_down = bell_draw(seeds[12], (EXPERTS, FF, MODEL_DIMENSION), (max(FF // 16, 1)) ** -0.5, 1.0, ((0, 4),))
    cotangent = bell_draw(seeds[13], (TOKENS, MODEL_DIMENSION), 1.0, 6.0, ((0, 32),))
    return {"tokens": tokens, "segments": segments, "routes": routes, "norm1_gain": norm1_gain, "w_query": w_query, "key_projection": key_projection, "value_projection": value_projection, "w_output": w_output, "norm2_gain": norm2_gain, "w_router": w_router, "expert_gate": expert_gate, "expert_up": expert_up, "expert_down": expert_down, "cotangent": cotangent}


EPSILON = 1e-06
ROPE_BASE = 10000.0
PRECISE = lax.Precision.HIGHEST

@jax.custom_vjp
def reduced_precision(v):
    return lax.optimization_barrier(v.astype(jnp.bfloat16)).astype(jnp.float32)

@jax.custom_vjp
def low_back(v):
    return v

def low_keep(v):
    return (reduced_precision(v), None)

def low_pass(kept, grad):
    return (grad,)

def back_keep(v):
    return (v, None)

def back_low(kept, grad):
    return (reduced_precision(grad),)
reduced_precision.defvjp(low_keep, low_pass)
low_back.defvjp(back_keep, back_low)

def rms_scale(values_in):
    return lax.rsqrt(lax.optimization_barrier(jnp.mean(values_in * values_in, axis=-1, keepdims=True)) + EPSILON)

def rotary_tables(sequence_length, head_size):
    half_size = head_size // 2
    exponent = jnp.arange(half_size, dtype=jnp.float32) * (2.0 / head_size)
    frequency = ROPE_BASE ** (-exponent)
    angles = jnp.arange(sequence_length, dtype=jnp.float32)[:, None] * frequency[None, :]
    return (jnp.cos(angles), jnp.sin(angles))

def rotate_pairs(field, cosine_table, sine_table):
    half_size = field.shape[-1] // 2
    first_half = field[..., :half_size]
    second_half = field[..., half_size:]
    return jnp.concatenate([first_half * cosine_table - second_half * sine_table, second_half * cosine_table + first_half * sine_table], axis=-1)

def attend_block(block_in):
    query_rows, rotated_keys, value_per_head, segment_ids = block_in
    sequence_length = query_rows.shape[0]
    grouped_heads = query_rows.reshape(sequence_length, KEY_VALUE_HEADS, QUERY_HEADS // KEY_VALUE_HEADS, HEAD_DIMENSION)
    scores = jnp.einsum('qkgd,skd->kgqs', grouped_heads, rotated_keys, precision=PRECISE) * (1.0 / math.sqrt(HEAD_DIMENSION))
    scores = low_back(scores)
    position = jnp.arange(sequence_length, dtype=jnp.int32)
    allowed = (segment_ids[:, None] == segment_ids[None, :]) & (position[:, None] >= position[None, :])
    scores = jnp.where(allowed, scores, -1e+30)
    weights_b = reduced_precision(jax.nn.softmax(scores, axis=-1))
    attended = jnp.einsum('kgqs,skd->qkgd', weights_b, value_per_head, precision=PRECISE)
    return attended.reshape(sequence_length, QUERY_HEADS * HEAD_DIMENSION)

def expert_term(normed_two, weight, gate_mat, up_mat, down_mat):
    copied = low_back(normed_two)
    gate_pre = low_back(jnp.dot(copied, gate_mat, precision=PRECISE))
    up_pre = low_back(jnp.dot(copied, up_mat, precision=PRECISE))
    hidden = reduced_precision(jax.nn.silu(gate_pre) * up_pre)
    expert_out = reduced_precision(low_back(jnp.dot(hidden, down_mat, precision=PRECISE)))
    return weight[:, None] * expert_out

def forward(inputs, gain_one, query_w, key_matrix, value_matrix, output_matrix, gain_two, router_w, gate_w, up_w, down_w, routes, segments):
    row_total = inputs.shape[0]
    blocks = row_total // TOK_DEV
    unit_one = inputs * rms_scale(inputs)
    first_normalized = reduced_precision(unit_one * gain_one)
    cosine_table, sine_table = rotary_tables(TOK_DEV, HEAD_DIMENSION)
    cosine_table = cosine_table[:, None, :]
    sine_table = sine_table[:, None, :]

    def apply_projection(weight_mat, heads):
        return low_back(jnp.dot(first_normalized, weight_mat, precision=PRECISE)).reshape(blocks, TOK_DEV, heads, HEAD_DIMENSION)
    query_rows = reduced_precision(rotate_pairs(apply_projection(query_w, QUERY_HEADS), cosine_table, sine_table))
    rotated_keys = reduced_precision(rotate_pairs(apply_projection(key_matrix, KEY_VALUE_HEADS), cosine_table, sine_table))
    value_per_head = reduced_precision(apply_projection(value_matrix, KEY_VALUE_HEADS))
    attended = lax.map(jax.checkpoint(attend_block), (query_rows, rotated_keys, value_per_head, segments.reshape(blocks, TOK_DEV)))
    attended = reduced_precision(low_back(attended.reshape(row_total, QUERY_HEADS * HEAD_DIMENSION)))
    after_attn = inputs + low_back(jnp.dot(attended, output_matrix, precision=PRECISE))
    unit_two = after_attn * rms_scale(after_attn)
    normed_two = reduced_precision(unit_two * gain_two)
    logits = jnp.dot(normed_two, router_w, precision=PRECISE)
    chosen = jnp.take_along_axis(logits, routes, axis=1)
    shares = jax.nn.softmax(chosen, axis=-1)

    def add_expert(running, expert_piece):
        expert_index, gate_mat, up_mat, down_mat = expert_piece
        weight = lax.optimization_barrier(jnp.sum(jnp.where(routes == expert_index, shares, 0.0), axis=1))
        running = running + jax.checkpoint(expert_term)(normed_two, weight, gate_mat, up_mat, down_mat)
        return (running, None)
    mixture, _ = lax.scan(add_expert, jnp.zeros(inputs.shape, jnp.float32), (jnp.arange(EXPERTS, dtype=jnp.int32), gate_w, up_w, down_w))
    return after_attn + mixture

def reference(tokens, segments, routes, norm1_gain, w_query, key_projection, value_projection, w_output, norm2_gain, w_router, expert_gate, expert_up, expert_down, cotangent):
    params = (tokens.astype(jnp.float32), norm1_gain.astype(jnp.float32), w_query.astype(jnp.float32), key_projection.astype(jnp.float32), value_projection.astype(jnp.float32), w_output.astype(jnp.float32), norm2_gain.astype(jnp.float32), w_router.astype(jnp.float32), expert_gate.astype(jnp.float32), expert_up.astype(jnp.float32), expert_down.astype(jnp.float32))

    def closed(*args_in):
        return forward(*args_in, routes, segments)
    result, pullback = jax.vjp(closed, *params)
    gradients = pullback(cotangent.astype(jnp.float32))
    return (result.astype(jnp.bfloat16), gradients[0], gradients[1], gradients[2], gradients[3], gradients[4], gradients[5], gradients[6], gradients[7], gradients[8], gradients[9], gradients[10])
```

```python
import math

import jax
import jax.numpy as jnp
from jax import lax
from jax.experimental import pallas as pl
from jax.experimental.pallas import tpu as pltpu
from jax.sharding import PartitionSpec as P

QUERY_HEADS = 16
KEY_VALUE_HEADS = 8
HEAD_DIMENSION = 64
EXPERTS = 32
EPSILON = 1e-06
ROPE_BASE = 10000.0
BF = jnp.bfloat16
F32 = jnp.float32


def rms_scale(values_in):
    return lax.rsqrt(jnp.mean(values_in * values_in, axis=-1, keepdims=True) + EPSILON)


def rotary_tables(sequence_length, head_size):
    half_size = head_size // 2
    exponent = jnp.arange(half_size, dtype=F32) * (2.0 / head_size)
    frequency = ROPE_BASE ** (-exponent)
    angles = jnp.arange(sequence_length, dtype=F32)[:, None] * frequency[None, :]
    return (jnp.cos(angles), jnp.sin(angles))


def rotate_pairs(field, cosine_table, sine_table):
    half_size = field.shape[-1] // 2
    first_half = field[..., :half_size]
    second_half = field[..., half_size:]
    return jnp.concatenate(
        [
            first_half * cosine_table - second_half * sine_table,
            second_half * cosine_table + first_half * sine_table,
        ],
        axis=-1,
    )


def contract_rows(left_side, right_side):
    return lax.dot_general(
        left_side, right_side, (((0,), (0,)), ((), ())), preferred_element_type=F32
    )


def contract_final_axis(left_side, right_side):
    return lax.dot_general(
        left_side, right_side, (((1,), (1,)), ((), ())), preferred_element_type=F32
    )


def matmul(left_side, right_side):
    return jnp.dot(left_side, right_side, preferred_element_type=F32)


def norm_backward(grad_normed, unit_part, scale_part, gain_part):
    grad_gain = jnp.sum(grad_normed * unit_part, axis=0)
    scaled = grad_normed * gain_part
    grad_in = scale_part * (
        scaled - unit_part * jnp.mean(scaled * unit_part, axis=-1, keepdims=True)
    )
    return (grad_gain, grad_in)


def swap(field, axis, bit):
    size = lax.axis_size(axis)
    return lax.ppermute(field, axis, [(i, i ^ bit) for i in range(size)])


def bit_order(size):
    bits = size.bit_length() - 1
    return [sum(((j >> b) & 1) << (bits - 1 - b) for b in range(bits)) for j in range(size)]


def gather_blocks(field, axis):
    size = lax.axis_size(axis)
    out = field[None]
    bit = 1
    while bit < size:
        out = jnp.concatenate([out, swap(out, axis, bit)], axis=0)
        bit *= 2
    return out


def gather_blocks_reversed(field, axis):
    size = lax.axis_size(axis)
    out = field[None]
    bit = size // 2
    while bit:
        out = jnp.concatenate([out, swap(out, axis, bit)], axis=0)
        bit //= 2
    order = bit_order(size)
    return jnp.stack([out[order[j]] for j in range(size)])


def gather_split(field, axis):
    half = field.shape[-1] // 2
    return jnp.concatenate(
        [
            gather_blocks(field[:, :half], axis),
            gather_blocks_reversed(field[:, half:], axis),
        ],
        axis=-1,
    )


def scatter_blocks(field, axis, wire):
    size = field.shape[0]
    bit = size // 2
    while bit:
        field = field[:bit] + swap(field[bit:].astype(wire), axis, bit).astype(F32)
        bit //= 2
    return field[0]


def scatter_blocks_reversed(field, axis, wire):
    size = field.shape[0]
    order = bit_order(size)
    field = jnp.stack([field[order[j]] for j in range(size)])
    half = size // 2
    bit = 1
    while bit < size:
        field = field[:half] + swap(field[half:].astype(wire), axis, bit).astype(F32)
        half //= 2
        bit *= 2
    return field[0]


def scatter_split(field, axis, wire):
    half = field.shape[-1] // 2
    return jnp.concatenate(
        [
            scatter_blocks(field[..., :half], axis, wire),
            scatter_blocks_reversed(field[..., half:], axis, wire),
        ],
        axis=-1,
    )


def core_pairs(z_pairs):
    return [(2 * a + c, 2 * b + c) for a, b in z_pairs for c in range(2)]


def line_sum(field):
    chips = lax.axis_size("dp") // 2
    chip = lax.axis_index("dp") // 2
    middle = chips // 2
    if chips == 1:
        return field
    for k in range(middle - 1):
        field = field + lax.ppermute(
            field, "dp", core_pairs([(k, k + 1), (chips - 1 - k, chips - 2 - k)])
        )
    field = field + lax.ppermute(
        field, "dp", core_pairs([(middle - 1, middle), (middle, middle - 1)])
    )
    for k in range(middle - 2, -1, -1):
        back = lax.ppermute(
            field, "dp", core_pairs([(k + 1, k), (chips - 2 - k, chips - 1 - k)])
        )
        field = jnp.where((chip == k) | (chip == chips - 1 - k), back, field)
    return field


def expert_kernel(first, last_tile):
    def body(ids, x, xt, dy, dyt, share, wg, wu, wd, *rest):
        if first:
            br_o, dn_o, ds_o, gg_o, gu_o, gd_o, ag, au, ad = rest
        else:
            br_i, dn_i, ds_i, br_o, dn_o, ds_o, gg_o, gu_o, gd_o, ag, au, ad = rest
        step = pl.program_id(0)
        rows = x[...]
        up_rows = dy[...]
        wgm = wg[0]
        wum = wu[0]
        wdm = wd[0]
        lane = lax.broadcasted_iota(jnp.int32, share.shape, 1)
        mine = lane == ids[1]
        w = jnp.sum(jnp.where(mine, share[...], 0.0), axis=1, keepdims=True)
        g = matmul(rows, wgm)
        u = matmul(rows, wum)
        t = contract_final_axis(up_rows, wdm)
        sig = 1.0 / (1.0 + jnp.exp(-g))
        sw = g * sig
        h = sw * u
        ds = jnp.sum(h * t, axis=1, keepdims=True)
        wh = (w * h).astype(BF)
        dh = w * t
        dg = (dh * u * sig * (1.0 + g * (1.0 - sig))).astype(BF)
        du = (dh * sw).astype(BF)
        br = matmul(wh, wdm)
        dn = contract_final_axis(dg, wgm) + contract_final_axis(du, wum)
        dsm = jnp.where(mine, ds, 0.0)
        if first:
            br_o[...] = br
            dn_o[...] = dn
            ds_o[...] = dsm
        else:
            br_o[...] = br_i[...] + br
            dn_o[...] = dn_i[...] + dn
            ds_o[...] = ds_i[...] + dsm
        pg = matmul(xt[...], dg)
        pu = matmul(xt[...], du)
        pd = matmul(dyt[...], wh)

        @pl.when(step == 0)
        def _():
            ag[...] = pg
            au[...] = pu
            ad[...] = pd

        @pl.when(step > 0)
        def _():
            ag[...] += pg
            au[...] += pu
            ad[...] += pd

        @pl.when(step == last_tile)
        def _():
            gg_o[...] = ag[...].astype(BF)
            gu_o[...] = au[...].astype(BF)
            gd_o[...] = ad[...].T.astype(BF)

    return body


def run_expert(ids, x, xt, dy, dyt, share, wg, wu, wd, carried, tile):
    rows, width = x.shape
    hidden_width = wg.shape[2]
    first = carried is None
    tiles = rows // tile
    row = lambda c: pl.BlockSpec((tile, c), lambda i, ids: (i, 0))
    col = lambda: pl.BlockSpec((width, tile), lambda i, ids: (0, i))
    whole = lambda s: pl.BlockSpec((1,) + s, lambda i, ids: (ids[0], 0, 0))
    const = lambda s: pl.BlockSpec(s, lambda i, ids: (0, 0))
    sums = [row(width), row(width), row(share.shape[1])]
    in_specs = [
        row(width),
        col(),
        row(width),
        col(),
        row(share.shape[1]),
        whole((width, hidden_width)),
        whole((width, hidden_width)),
        whole((hidden_width, width)),
    ] + ([] if first else sums)
    sds = jax.ShapeDtypeStruct
    return pl.pallas_call(
        expert_kernel(first, tiles - 1),
        out_shape=(
            sds((rows, width), F32),
            sds((rows, width), F32),
            sds(share.shape, F32),
            sds((width, hidden_width), BF),
            sds((width, hidden_width), BF),
            sds((hidden_width, width), BF),
        ),
        grid_spec=pltpu.PrefetchScalarGridSpec(
            num_scalar_prefetch=1,
            grid=(tiles,),
            in_specs=in_specs,
            out_specs=sums
            + [
                const((width, hidden_width)),
                const((width, hidden_width)),
                const((hidden_width, width)),
            ],
            scratch_shapes=[pltpu.VMEM((width, hidden_width), F32)] * 3,
        ),
        input_output_aliases={} if first else {9: 0, 10: 1, 11: 2},
        compiler_params=pltpu.CompilerParams(
            dimension_semantics=("arbitrary",), vmem_limit_bytes=56 << 20
        ),
        cost_estimate=pl.CostEstimate(
            flops=18 * rows * width * hidden_width,
            bytes_accessed=rows * width * 24,
            transcendentals=rows * hidden_width,
        ),
        name="expert_all",
    )(ids, x, xt, dy, dyt, share, wg, wu, wd, *(() if first else carried))


def place_kernel(ids, own, other, *rest):
    out = rest[-1]
    step = pl.program_id(0)

    @pl.when(step == 0)
    def _():
        out[0] = own[...].astype(F32)

    @pl.when(step == 1)
    def _():
        out[0] = other[...].astype(F32)


def place(ids, own, other, total, previous):
    r, c = own.shape
    const = pl.BlockSpec((r, c), lambda i, ids: (0, 0))
    return pl.pallas_call(
        place_kernel,
        out_shape=jax.ShapeDtypeStruct((total, r, c), F32),
        grid_spec=pltpu.PrefetchScalarGridSpec(
            num_scalar_prefetch=1,
            grid=(2,),
            in_specs=[const, const]
            + ([] if previous is None else [pl.BlockSpec(memory_space=pl.ANY)]),
            out_specs=pl.BlockSpec((1, r, c), lambda i, ids: (ids[i], 0, 0)),
        ),
        input_output_aliases={} if previous is None else {3: 0},
        compiler_params=pltpu.CompilerParams(dimension_semantics=("arbitrary",)),
        name="place",
    )(ids, own, other, *(() if previous is None else (previous,)))


def shards(
    tokens,
    segments,
    routes,
    norm1_gain,
    w_query,
    key_projection,
    value_projection,
    w_output,
    norm2_gain,
    w_router,
    expert_gate,
    expert_up,
    expert_down,
    cotangent,
):
    n, width = tokens.shape
    local_count = expert_gate.shape[0]
    per_core = local_count // 2
    owners = lax.axis_size("expert")
    core = lax.axis_index("dp") % 2
    owner = lax.axis_index("expert")
    group_width = QUERY_HEADS // KEY_VALUE_HEADS
    kv_width = KEY_VALUE_HEADS * HEAD_DIMENSION
    score_scale = 1.0 / math.sqrt(HEAD_DIMENSION)
    shard_rows = w_query.shape[0]

    pad = lambda c: jnp.zeros((shard_rows, c), BF)
    first_pack = jnp.concatenate(
        [w_query, key_projection, value_projection, norm1_gain[:, None], pad(127)], axis=1
    )
    second_pack = jnp.concatenate(
        [w_output, w_router, norm2_gain[:, None], pad(95)], axis=1
    )
    first_pack = lax.all_gather(first_pack, "dp", axis=0, tiled=True)
    second_pack = lax.all_gather(second_pack, "dp", axis=0, tiled=True)
    qkv_width = width + 2 * kv_width
    qkv_matrix = first_pack[:, :qkv_width]
    gain_one = first_pack[:, qkv_width].astype(F32)[None, :]
    output_matrix = second_pack[:, :width]
    router_w = second_pack[:, width : width + EXPERTS]
    gain_two = second_pack[:, width + EXPERTS].astype(F32)[None, :]

    dy_group = gather_split(cotangent, "expert").reshape(owners * n, width)
    dy_all = jnp.concatenate([dy_group, swap(dy_group, "dp", 1)], axis=0)
    dy_all_t = dy_all.T

    inputs = tokens.astype(F32)
    scale_one = rms_scale(inputs)
    unit_one = inputs * scale_one
    first_normalized = (unit_one * gain_one).astype(BF)
    cosine_table, sine_table = rotary_tables(n, HEAD_DIMENSION)
    cosine_table = cosine_table[:, None, :]
    sine_table = sine_table[:, None, :]
    qkv = matmul(first_normalized, qkv_matrix)
    query_rows = rotate_pairs(
        qkv[:, :width].reshape(n, QUERY_HEADS, HEAD_DIMENSION), cosine_table, sine_table
    )
    query_rows = query_rows.astype(BF).reshape(n, KEY_VALUE_HEADS, group_width, HEAD_DIMENSION)
    rotated_keys = rotate_pairs(
        qkv[:, width : width + kv_width].reshape(n, KEY_VALUE_HEADS, HEAD_DIMENSION),
        cosine_table,
        sine_table,
    ).astype(BF)
    value_per_head = (
        qkv[:, width + kv_width :].astype(BF).reshape(n, KEY_VALUE_HEADS, HEAD_DIMENSION)
    )
    position = jnp.arange(n, dtype=jnp.int32)
    allowed = (segments[:, None] == segments[None, :]) & (position[:, None] >= position[None, :])

    def score_block():
        raw_scores = (
            jnp.einsum("qkgd,skd->kgqs", query_rows, rotated_keys, preferred_element_type=F32)
            * score_scale
        )
        return jnp.where(allowed, raw_scores, -1e30)

    scores = score_block()
    row_peak = jnp.max(scores, axis=-1, keepdims=True)
    log_total = row_peak + jnp.log(jnp.sum(jnp.exp(scores - row_peak), axis=-1, keepdims=True))
    weights_b = jnp.exp(scores - log_total).astype(BF)
    attended = jnp.einsum("kgqs,skd->qkgd", weights_b, value_per_head, preferred_element_type=F32)
    attended = attended.astype(BF).reshape(n, QUERY_HEADS * HEAD_DIMENSION)
    after_attn = inputs + matmul(attended, output_matrix)
    scale_two = rms_scale(after_attn)
    unit_two = after_attn * scale_two
    normed_two = (unit_two * gain_two).astype(BF)

    rows_group = gather_split(normed_two, "expert").reshape(owners * n, width)
    rows_all = jnp.concatenate([rows_group, swap(rows_group, "dp", 1)], axis=0)
    rows_all_t = rows_all.T

    logits = matmul(normed_two, router_w)
    expert_ids = jnp.arange(EXPERTS, dtype=jnp.int32)
    chosen = jnp.any(routes[:, :, None] == expert_ids[None, None, :], axis=1)
    masked = jnp.where(chosen, logits, -jnp.inf)
    weight = jnp.where(
        chosen, jnp.exp(logits - jnp.max(masked, axis=-1, keepdims=True)), 0.0
    )
    shares = weight / jnp.sum(weight, axis=-1, keepdims=True)
    share_group = gather_blocks(shares, "expert").reshape(owners * n, EXPERTS)
    share_all = jnp.concatenate([share_group, swap(share_group, "dp", 1)], axis=0)

    carried = None
    made = []
    for e in range(per_core):
        local = core * per_core + e
        ids = jnp.stack([local, owner * local_count + local]).astype(jnp.int32)
        out = run_expert(
            ids,
            rows_all,
            rows_all_t,
            dy_all,
            dy_all_t,
            share_all,
            expert_gate,
            expert_up,
            expert_down,
            carried,
            n,
        )
        carried = out[:3]
        made.append(out[3:])
    branch_all, dn2_all, dshare_all = carried

    def to_tokens(field, wire, split):
        half = owners * n
        own = field[:half] + swap(field[half:].astype(wire), "dp", 1).astype(F32)
        own = own.reshape(owners, n, field.shape[1])
        return (scatter_split if split else scatter_blocks)(own, "expert", wire)

    dn2_moe = to_tokens(dn2_all, BF, True)
    dshare = to_tokens(dshare_all, F32, False)
    output = (after_attn + to_tokens(branch_all, BF, True)).astype(BF)

    slabs = jnp.stack([core * per_core, (1 - core) * per_core]).astype(jnp.int32)
    expert_totals = [None, None, None]
    for e in range(per_core):
        for m in range(3):
            total = line_sum(made[e][m])
            expert_totals[m] = place(
                slabs + e, total, swap(total, "dp", 1), local_count, expert_totals[m]
            )

    upstream = cotangent.astype(F32)
    dlogits = shares * (dshare - jnp.sum(shares * dshare, axis=-1, keepdims=True))
    dlogits = dlogits.astype(BF)
    grad_router = contract_rows(normed_two, dlogits)
    dn2 = dn2_moe + contract_final_axis(dlogits, router_w)
    grad_gain_two, dx2_norm = norm_backward(dn2, unit_two, scale_two, gain_two)
    dx2 = upstream + dx2_norm
    grad_attention_output = dx2.astype(BF)
    grad_output = contract_rows(attended, grad_attention_output)
    dmixed = (
        contract_final_axis(grad_attention_output, output_matrix)
        .astype(BF)
        .reshape(n, KEY_VALUE_HEADS, group_width, HEAD_DIMENSION)
    )
    scores_again = score_block()
    probs_back = jnp.exp(scores_again - log_total)
    dprob = jnp.einsum("qkgd,skd->kgqs", dmixed, value_per_head, preferred_element_type=F32)
    value_gradient = jnp.einsum(
        "kgqs,qkgd->skd", probs_back.astype(BF), dmixed, preferred_element_type=F32
    )
    value_gradient = value_gradient.astype(BF).reshape(n, kv_width)
    dscore = (probs_back * (dprob - jnp.sum(probs_back * dprob, axis=-1, keepdims=True))).astype(
        BF
    )
    dquery = (
        jnp.einsum("kgqs,skd->qkgd", dscore, rotated_keys, preferred_element_type=F32)
        * score_scale
    )
    dquery = (
        rotate_pairs(
            dquery.reshape(n, QUERY_HEADS, HEAD_DIMENSION), cosine_table, -sine_table
        )
        .astype(BF)
        .reshape(n, QUERY_HEADS * HEAD_DIMENSION)
    )
    key_gradient = (
        jnp.einsum("kgqs,qkgd->skd", dscore, query_rows, preferred_element_type=F32)
        * score_scale
    )
    key_gradient = (
        rotate_pairs(key_gradient, cosine_table, -sine_table).astype(BF).reshape(n, kv_width)
    )
    dqkv = jnp.concatenate([dquery, key_gradient, value_gradient], axis=1)
    grad_qkv = contract_rows(first_normalized, dqkv)
    dn1 = contract_final_axis(dqkv, qkv_matrix)
    grad_gain_one, dx_norm = norm_backward(dn1, unit_one, scale_one, gain_one)
    grad_tokens = dx2 + dx_norm

    mixer = jnp.concatenate(
        [
            grad_qkv.astype(BF),
            grad_output.astype(BF),
            grad_router.astype(BF),
            grad_gain_one.astype(BF)[:, None],
            grad_gain_two.astype(BF)[:, None],
            jnp.zeros((width, 94), BF),
        ],
        axis=1,
    )
    mixer = lax.psum_scatter(mixer, "expert", scatter_dimension=1, tiled=True)
    mixer = lax.psum_scatter(mixer, "dp", scatter_dimension=0, tiled=True)
    mixer = lax.all_gather(mixer, "expert", axis=1, tiled=True).astype(F32)
    at = qkv_width + width
    return (
        output,
        grad_tokens,
        mixer[:, at + EXPERTS],
        mixer[:, :width],
        mixer[:, width : width + kv_width],
        mixer[:, width + kv_width : qkv_width],
        mixer[:, qkv_width:at],
        mixer[:, at + EXPERTS + 1],
        mixer[:, at : at + EXPERTS],
        expert_totals[0],
        expert_totals[1],
        expert_totals[2],
    )


def solution(mesh):
    both = ("dp", "expert")
    placed = (
        P(both, None),
        P(both),
        P(both, None),
        P("dp"),
        P("dp", None),
        P("dp", None),
        P("dp", None),
        P("dp", None),
        P("dp"),
        P("dp", None),
        P("expert", None, None),
        P("expert", None, None),
        P("expert", None, None),
        P(both, None),
    )
    return jax.shard_map(
        shards,
        mesh=mesh,
        in_specs=placed,
        out_specs=(
            P(both, None),
            P(both, None),
            P("dp"),
            P("dp", None),
            P("dp", None),
            P("dp", None),
            P("dp", None),
            P("dp"),
            P("dp", None),
            P("expert", None, None),
            P("expert", None, None),
            P("expert", None, None),
        ),
        check_vma=False,
    )
```
